512 devices in a mesh: ctx: 64 (over z, y_hi, x), head: 8 (over y_lo, core).
Axes of the slice: x: 4, y: 8 (y_hi: 2, y_lo: 4; y = y_hi * 4 + y_lo), z: 8, core: 2. Of those that a mesh axis runs over, the one named last changes fastest.
Arguments:
- hidden: bfloat16 [32768, 4096], P('ctx', 'head'), may hold values from -6 to 6
- w_query: bfloat16 [4096, 2048], P(None, 'head'), may hold values from -0.09375 to 0.09375
- keys: bfloat16 [32768, 2048], P('ctx', 'head'), may hold values from -6 to 6
- values: bfloat16 [32768, 2048], P('ctx', 'head'), may hold values from -6 to 6
- d_out: bfloat16 [32768, 2048], P('ctx', 'head'), may hold values from -6 to 6
- log_decay: float32 [32768, 16], P('ctx', 'head'), may hold values from -1.5 to 0, as said below
Outputs:
- d_hidden: bfloat16 [32768, 4096], P('ctx', 'head')
- d_keys: bfloat16 [32768, 2048], P('ctx', 'head')
- d_values: bfloat16 [32768, 2048], P('ctx', 'head')
The draws below stay inside these ranges and needn't reach their ends.
Inputs may be any that keep to these rules, and one draw needn't show every extreme that they name: `log_decay`: every entry is negative.
All inputs are finite; a program needn't handle non-finite values.
Results may differ from the reference program's by a relative error of at most 0.013.
Values may be sent and summed in bfloat16 or wider, within the bound.
A program may use at most 64 MiB of HBM per device.

```python
import math
import jax
import jax.numpy as jnp
from jax import lax

D = 4096
HDIM = 128
HEAD_GROUP = 16
TOK_DEV = 512
TOKEN_COUNT = 32768
N_CTX = 64
N_HEAD = 8


def draw_log_decay(key, part):
    draw_keys = jax.random.split(key, 7)
    fast_share = 0.5
    picker = jax.random.uniform(draw_keys[0], (HEAD_GROUP,))
    fast_rate = jnp.exp(jax.random.uniform(draw_keys[1], (HEAD_GROUP,), minval=math.log(1.0 / 50.0), maxval=math.log(1.0 / 30.0)))
    slow_rate = jnp.exp(jax.random.uniform(draw_keys[2], (HEAD_GROUP,), minval=math.log(0.1), maxval=math.log(0.5))) / TOKEN_COUNT
    head_decay_rate = jnp.where(picker < fast_share, fast_rate, slow_rate)
    jaggedness = jnp.exp(jax.random.uniform(draw_keys[3], (TOKEN_COUNT, HEAD_GROUP), minval=-math.log(2.0), maxval=math.log(2.0)))
    block_count = TOKEN_COUNT // TOK_DEV
    block_local = jnp.exp(jax.random.uniform(draw_keys[4], (block_count, HEAD_GROUP), minval=-math.log(2.0), maxval=math.log(2.0)))
    block_local = jnp.repeat(block_local, TOK_DEV, axis=0)
    spike_positions = jax.random.randint(draw_keys[5], (3, HEAD_GROUP), 0, TOKEN_COUNT)
    spike_loss = jax.random.uniform(draw_keys[6], (3, HEAD_GROUP), minval=0.2, maxval=0.35)
    match_flags = jnp.arange(TOKEN_COUNT)[:, None, None] == spike_positions[None]
    spike_events = jnp.sum(jnp.where(match_flags, jnp.log1p(-spike_loss)[None], 0.0), axis=1)
    return (-head_decay_rate[None] * jaggedness * block_local + spike_events).astype(jnp.float32)


def steps_of(key, dims, pieces, low, largest):
    loudness, own = 1.0, jax.random.fold_in(key, 6)
    for dim, blocks in pieces:
        heights = jnp.exp(jax.random.uniform(jax.random.fold_in(own, dim), (blocks,), jnp.float32, low / len(pieces), largest / len(pieces)))
        loudness = loudness * jnp.repeat(heights, dims[dim] // blocks).reshape([-1 if axis == dim else 1 for axis in range(len(dims))])
    return loudness


def gaussian(rng, dims, scale, most, cuts=(), kind=jnp.bfloat16):
    array = scale * jax.random.normal(rng, dims, jnp.float32)
    if cuts:
        array = array * steps_of(rng, dims, cuts, -0.22, 0.18)
    return jnp.clip(array, -most, most).astype(kind)


def setup_inputs(seed: int = 0) -> dict:
    key_list = jax.random.split(jax.random.key(seed), 7)
    return {
        "hidden": gaussian(key_list[0], (TOKEN_COUNT, D), 1.0, 6.0, ((0, 64), (1, 8))),
        "w_query": gaussian(key_list[1], (D, HEAD_GROUP * HDIM), D ** -0.5, 0.09375, ((1, 8),)),
        "keys": gaussian(key_list[2], (TOKEN_COUNT, HEAD_GROUP * HDIM), 1.0, 6.0, ((0, 64), (1, 8))),
        "values": gaussian(key_list[3], (TOKEN_COUNT, HEAD_GROUP * HDIM), 1.0, 6.0, ((0, 64), (1, 8))),
        "d_out": gaussian(key_list[4], (TOKEN_COUNT, HEAD_GROUP * HDIM), 1.0, 6.0, ((0, 64), (1, 8))),
        "log_decay": draw_log_decay(jax.random.fold_in(key_list[6], 71), 0),
    }


highest = lax.Precision.HIGHEST

def rounded(value):
    return lax.optimization_barrier(value.astype(jnp.bfloat16)).astype(jnp.float32)

def summaries(query_heads, scaled_keys, value_heads, grad_heads, cumulative, block_total, scaling):
    keep_share = jnp.exp(block_total[None] - cumulative)[:, :, None]
    decayed_keys = rounded(keep_share * scaled_keys.astype(jnp.float32))
    local_state = jnp.einsum('bhe,bhf->hef', decayed_keys, value_heads.astype(jnp.float32))
    decayed_queries = rounded(scaling * jnp.exp(cumulative)[:, :, None] * query_heads.astype(jnp.float32))
    local_adjoint = jnp.einsum('bhe,bhf->hef', decayed_queries, grad_heads.astype(jnp.float32))
    return (local_state, local_adjoint)

def gradients(query_heads, scaled_keys, value_heads, grad_heads, gate_gain, cumulative, block_total, state_in, adjoint_in, scaling):
    row_count = query_heads.shape[0]
    places = jnp.arange(row_count)
    causal = (places[:, None] >= places[None, :])[None]
    cumul_heads = cumulative.T
    spread = cumul_heads[:, :, None] - cumul_heads[:, None, :]
    decays = jnp.where(causal, jnp.exp(jnp.where(causal, spread, 0.0)), 0.0) * scaling
    query_wide = query_heads.astype(jnp.float32)
    keys_wide = scaled_keys.astype(jnp.float32)
    values_wide = value_heads.astype(jnp.float32)
    grads_wide = grad_heads.astype(jnp.float32)
    weight_dv = rounded(decays * jnp.einsum('the,she->hts', grads_wide, values_wide))
    weight_kq = rounded(decays * jnp.einsum('the,she->hts', query_wide, keys_wide))
    carry_query = jnp.einsum('thf,hef->the', grads_wide, state_in, precision=highest)
    d_query = jnp.einsum('hts,she->the', weight_dv, keys_wide) + scaling * jnp.exp(cumulative)[:, :, None] * carry_query
    tail_decay = jnp.exp(block_total[None] - cumulative)[:, :, None]
    carry_keys = jnp.einsum('shf,hef->she', values_wide, adjoint_in, precision=highest)
    carry_values = jnp.einsum('she,hef->shf', keys_wide, adjoint_in, precision=highest)
    d_scaled = jnp.einsum('hts,the->she', weight_dv, query_wide) + tail_decay * carry_keys
    d_values = jnp.einsum('hts,the->she', weight_kq, grads_wide) + tail_decay * carry_values
    d_keys = gate_gain[:, :, None] * d_scaled
    return (d_query.astype(jnp.bfloat16), d_keys.astype(jnp.bfloat16), d_values.astype(jnp.bfloat16))

def reference(hidden, w_query, keys, values, d_out, log_decay):
    scaling = HDIM ** (-0.5)
    query = jnp.dot(hidden, w_query, preferred_element_type=jnp.float32).astype(jnp.bfloat16)
    gate_gain = jnp.sqrt(-jnp.expm1(2.0 * log_decay))
    head_shape = (N_CTX, TOK_DEV, HEAD_GROUP, HDIM)
    gain_blocks = gate_gain.reshape(N_CTX, TOK_DEV, HEAD_GROUP)
    query_heads = query.reshape(head_shape)
    scaled_keys = (gain_blocks[..., None] * keys.reshape(head_shape).astype(jnp.float32)).astype(jnp.bfloat16)
    value_heads = values.reshape(head_shape)
    grad_heads = d_out.reshape(head_shape)
    cumulative = jnp.cumsum(log_decay.reshape(N_CTX, TOK_DEV, HEAD_GROUP), axis=1)
    block_total = cumulative[:, -1]
    local_state, local_adjoint = lax.map(lambda items: summaries(*items, scaling), (query_heads, scaled_keys, value_heads, grad_heads, cumulative, block_total))
    zero_states = jnp.zeros((HEAD_GROUP, HDIM, HDIM), jnp.float32)

    def advance(carried, item):
        total_log, local_part = item
        return (jnp.exp(total_log)[:, None, None] * carried + local_part, carried)
    _, state_in = lax.scan(advance, zero_states, (block_total, local_state))
    _, adjoint_in = lax.scan(advance, zero_states, (block_total, local_adjoint), reverse=True)
    d_query, d_keys, d_values = lax.map(lambda items: gradients(*items, scaling), (query_heads, scaled_keys, value_heads, grad_heads, gain_blocks, cumulative, block_total, state_in, adjoint_in))
    d_flat = d_query.reshape(TOKEN_COUNT, HEAD_GROUP * HDIM)
    group_width = HEAD_GROUP // N_HEAD * HDIM
    summed = jnp.zeros((TOKEN_COUNT, D), jnp.float32)
    for group_index in range(N_HEAD):
        low_col = group_index * group_width
        group_term = jnp.dot(d_flat[:, low_col:low_col + group_width], w_query[:, low_col:low_col + group_width].T, preferred_element_type=jnp.float32)
        summed = summed + rounded(group_term)
    d_hidden = summed.astype(jnp.bfloat16)
    return (d_hidden, d_keys.reshape(TOKEN_COUNT, HEAD_GROUP * HDIM), d_values.reshape(TOKEN_COUNT, HEAD_GROUP * HDIM))
```

```python
import functools

import jax
import jax.numpy as jnp
from jax import lax
from jax.experimental import pallas as pl
from jax.experimental.pallas import tpu as pltpu
from jax.sharding import PartitionSpec as P

MESH = pl.DeviceIdType.MESH
F32 = jnp.float32
BF16 = jnp.bfloat16
HDIM = 128
NX, NY, NZ = 4, 2, 8
NP = 4
QUARTER = HDIM // NX
OFFSETS = (2, -2, 1, -1)
AHEAD = 3


def mm(a, b):
    return lax.dot_general(a, b, (((1,), (0,)), ((), ())), preferred_element_type=F32)


def mm_nt(a, b):
    return lax.dot_general(a, b, (((1,), (1,)), ((), ())), preferred_element_type=F32)


def mm_tn(a, b):
    return lax.dot_general(a, b, (((0,), (0,)), ((), ())), preferred_element_type=F32)


def one_less_exp(x):
    series = jnp.full_like(x, 1.0)
    for n in range(9, 1, -1):
        series = 1.0 + x * (1.0 / n) * series
    return jnp.where(x > -0.5, -x * series, 1.0 - jnp.exp(x))


def kernel(
    hidden, w_hbm, keys, values, d_out, logs,
    dh_ref, dk_ref, dv_ref,
    hid, w, wr, dqf, query, sk, lg, rows, dec, wdv,
    loc, p1, p2, p3, p4s, p4, tx, by, bz, sums,
    in_sem,
    h_send, h_sib, h_fwd, h_rel, h_recv,
    q_send, q_sib, q_fwd, q_rel, q_recv,
    wy_send, wy_recv, wz_send, wz_recv, wx_send, wx_recv, wf_send, wf_recv,
    s1_send, s1_recv, s2_send, s2_recv, s3_send, s3_recv, s4_send, s4_recv,
    t1_send, t1_recv, t2_send, t2_recv, t3_send, t3_recv,
):
    scale = HDIM ** (-0.5)
    tokens = hidden.shape[0]
    feats = hidden.shape[1]
    width = w_hbm.shape[1]
    nhead = width // HDIM
    ctx, head = lax.axis_index("ctx"), lax.axis_index("head")
    x = lax.rem(ctx, NX)
    y = lax.rem(lax.div(ctx, NX), NY)
    z = lax.div(ctx, NX * NY)
    chip, core = lax.div(head, 2), lax.rem(head, 2)
    sib = 2 * chip + 1 - core

    def ctx_at(zz, yy, xx):
        return (zz * NY + yy) * NX + xx

    def to_head(other):
        return {"head": other}

    def to_ctx(other):
        return {"ctx": other}

    def remote(src, dst, send, recv, device):
        return pltpu.make_async_remote_copy(
            src_ref=src, dst_ref=dst, send_sem=send, recv_sem=recv,
            device_id=device, device_id_type=MESH,
        )

    def arrived(dst, sem):
        remote(dst, dst, sem, sem, to_head(sib)).wait_recv()

    pending = []

    def send(copy):
        copy.start()
        pending.append((None, copy))

    def send_if(cond, make):
        @pl.when(cond)
        def _():
            make().start()

        pending.append((cond, make))

    local = [
        pltpu.make_async_copy(hidden, hid.at[head], in_sem.at[0]),
        pltpu.make_async_copy(w_hbm, w, in_sem.at[1]),
    ]
    for copy in local:
        copy.start()

    barrier = pltpu.get_barrier_semaphore()
    partners = [to_head(lax.rem(head + d, 2 * NP)) for d in range(1, 2 * NP)]
    partners += [to_ctx(ctx_at(z, y, lax.rem(x + d, NX))) for d in range(1, NX)]
    partners += [to_ctx(ctx_at(z, 1 - y, x))]
    partners += [to_ctx(ctx_at(lax.rem(z + d, NZ), y, x)) for d in range(1, NZ)]
    for partner in partners:
        pl.semaphore_signal(barrier, inc=1, device_id=partner, device_id_type=MESH)
    pl.semaphore_wait(barrier, len(partners))

    part = feats // (NX * NZ)
    slot = pl.multiple_of((x * NZ + z) * part, part)

    def weights_y():
        local[1].wait()
        mine = w.at[pl.ds(pl.multiple_of(head * feats + slot, part), part), :]
        for d in range(1, 2 * NP):
            other = lax.rem(head + d, 2 * NP)
            send(remote(
                w.at[pl.ds(pl.multiple_of(other * feats + slot, part), part), :],
                wr.at[head, pl.ds(slot, part), :],
                wy_send.at[d - 1], wy_recv.at[head], to_head(other),
            ))
        wr[head, pl.ds(slot, part), :] = mine[...]

    def weights_z():
        for d in range(1, 2 * NP):
            other = lax.rem(head + d, 2 * NP)
            arrived(wr.at[other, pl.ds(slot, part), :], wy_recv.at[other])
        mine = wr.at[:, pl.ds(slot, part), :]
        for d in (4, 3, 5, 2, 6, 1, 7):
            send(remote(mine, mine, wz_send.at[d - 1], wz_recv.at[z],
                        to_ctx(ctx_at(lax.rem(z + d, NZ), y, x))))

    line = part * NZ
    right, left = lax.rem(x + 1, NX), lax.rem(x + NX - 1, NX)
    across = lax.rem(x + 2, NX)

    def line_of(xx):
        return pl.ds(pl.multiple_of(xx * line, line), line)

    def weights_x():
        for d in range(1, NZ):
            zz = lax.rem(z + d, NZ)
            arrived(wr.at[:, pl.ds(pl.multiple_of((x * NZ + zz) * part, part), part), :],
                    wz_recv.at[zz])
        mine = wr.at[:, line_of(x), :]
        send(remote(mine, mine, wx_send.at[0], wx_recv.at[0], to_ctx(ctx_at(z, y, right))))
        send(remote(mine, mine, wx_send.at[1], wx_recv.at[1], to_ctx(ctx_at(z, y, left))))

    def weights_forward():
        from_left = wr.at[:, line_of(left), :]
        arrived(from_left, wx_recv.at[0])
        half = wr.at[pl.ds(0, NP), line_of(left), :]
        send(remote(half, half, wf_send.at[0], wf_recv.at[0], to_ctx(ctx_at(z, y, right))))
        from_right = wr.at[:, line_of(right), :]
        arrived(from_right, wx_recv.at[1])
        half = wr.at[pl.ds(NP, NP), line_of(right), :]
        send(remote(half, half, wf_send.at[1], wf_recv.at[1], to_ctx(ctx_at(z, y, left))))

    def weights_end():
        arrived(wr.at[pl.ds(0, NP), line_of(across), :], wf_recv.at[0])
        arrived(wr.at[pl.ds(NP, NP), line_of(across), :], wf_recv.at[1])

    def gather(buf, step, s_send, s_sib, s_fwd, s_rel, s_recv):
        def piece(block, k):
            return buf.at[block, pl.ds(k * step, step), :]

        def issue(k):
            mine = piece(head, k)
            recv = s_recv.at[head, k]
            for i, d in enumerate(OFFSETS):
                other = chip + d
                ok = jnp.logical_and(other >= 0, other < NP)
                send_if(ok, functools.partial(
                    remote, mine, mine, s_send.at[i, k], recv, to_head(2 * other + core)))
            send(remote(mine, mine, s_sib.at[k], recv, to_head(sib)))

        def forward(k):
            for i, d in enumerate((2, 1, 3)):
                block = 2 * lax.rem(chip + d, NP) + core
                got = piece(block, k)
                recv = s_recv.at[block, k]
                arrived(got, recv)
                if d == 2:
                    ok = jnp.logical_and(chip >= 1, chip <= 2)
                    end = jnp.where(chip == 2, 3, 0)
                    send_if(ok, functools.partial(
                        remote, got, got, s_rel.at[k], recv, to_head(2 * end + core)))
                send(remote(got, got, s_fwd.at[i, k], recv, to_head(sib)))

        def finish(k):
            for d in range(NP):
                block = 2 * lax.rem(chip + d, NP) + 1 - core
                arrived(piece(block, k), s_recv.at[block, k])

        return issue, forward, finish

    h_step = tokens // h_sib.shape[0]
    q_step = tokens // q_sib.shape[0]
    h_issue, h_forward, h_finish = gather(hid, h_step, h_send, h_sib, h_fwd, h_rel, h_recv)
    q_issue, q_forward, q_finish = gather(dqf, q_step, q_send, q_sib, q_fwd, q_rel, q_recv)

    def line_fold(parts, gains, reverse, start):
        outs = [None] * len(parts)
        acc = start
        order = range(len(parts))
        for i in reversed(order) if reverse else order:
            outs[i] = acc
            acc = [gains[i][h] * acc[h] + parts[i][h] for h in range(nhead)]
        return outs, acc

    def zeros():
        return [jnp.zeros((QUARTER, HDIM), F32) for _ in range(nhead)]

    def gains_of(ref, count):
        return [[jnp.exp(ref[i][h : h + 1, :]) for h in range(nhead)] for i in range(count)]

    def parts_of(ref, n, count):
        return [[ref[n, i, h].astype(F32) for h in range(nhead)] for i in range(count)]

    def scan_x(n, states):
        for q in range(NX):
            for h in range(nhead):
                loc[n, q, h] = states[h][q * QUARTER : (q + 1) * QUARTER].astype(BF16)
        for d in (2, 1, 3):
            xx = lax.rem(x + d, NX)
            device = to_ctx(ctx_at(z, y, xx))
            send(remote(loc.at[n, xx], p1.at[n, x], s1_send.at[n, d - 1], s1_recv.at[n, x], device))
            if n == 0:
                send(remote(tx.at[x], tx.at[x], t1_send.at[d - 1], t1_recv.at[x], device))
        p1[n, x] = loc[n, x]

    def scan_y(n):
        for d in (1, 3, 2):
            xx = lax.rem(x + d, NX)
            arrived(p1.at[n, xx], s1_recv.at[n, xx])
            if n == 0:
                arrived(tx.at[xx], t1_recv.at[xx])
        if n == 0:
            by[y] = tx[0] + tx[1] + tx[2] + tx[3]
        _, total = line_fold(parts_of(p1, n, NX), gains_of(tx, NX), n == 1, zeros())
        for h in range(nhead):
            p2[n, y, h] = total[h].astype(BF16)
        device = to_ctx(ctx_at(z, 1 - y, x))
        send(remote(p2.at[n, y], p2.at[n, y], s2_send.at[n], s2_recv.at[n, y], device))
        if n == 0:
            send(remote(by.at[y], by.at[y], t2_send.at[0], t2_recv.at[y], device))

    def scan_z(n):
        arrived(p2.at[n, 1 - y], s2_recv.at[n, 1 - y])
        if n == 0:
            arrived(by.at[1 - y], t2_recv.at[1 - y])
            bz[z] = by[0] + by[1]
        _, total = line_fold(parts_of(p2, n, NY), gains_of(by, NY), n == 1, zeros())
        for h in range(nhead):
            p3[n, z, h] = total[h].astype(BF16)
        for d in (4, 3, 5, 2, 6, 1, 7):
            device = to_ctx(ctx_at(lax.rem(z + d, NZ), y, x))
            send(remote(p3.at[n, z], p3.at[n, z], s3_send.at[n, d - 1], s3_recv.at[n, z], device))
            if n == 0:
                send(remote(bz.at[z], bz.at[z], t3_send.at[d - 1], t3_recv.at[z], device))

    def scan_back(n):
        for d in (1, 7, 2, 6, 3, 5, 4):
            zz = lax.rem(z + d, NZ)
            arrived(p3.at[n, zz], s3_recv.at[n, zz])
            if n == 0:
                arrived(bz.at[zz], t3_recv.at[zz])
        reverse = n == 1
        gains = gains_of(bz, NZ)
        parts = parts_of(p3, n, NZ)
        acc = zeros()
        for i in reversed(range(NZ)) if reverse else range(NZ):
            use = z < i if reverse else z > i
            keep = jnp.where(use, 1.0, 0.0)
            acc = [
                acc[h] * (1.0 - keep + keep * gains[i][h]) + keep * parts[i][h]
                for h in range(nhead)
            ]
        outs, _ = line_fold(parts_of(p2, n, NY), gains_of(by, NY), reverse, acc)
        first = jnp.where(y == 0, 1.0, 0.0)
        acc = [first * outs[0][h] + (1.0 - first) * outs[1][h] for h in range(nhead)]
        outs, _ = line_fold(parts_of(p1, n, NX), gains_of(tx, NX), reverse, acc)
        for i in range(NX):
            for h in range(nhead):
                p4s[n, i, h] = outs[i][h].astype(BF16)
        for d in (2, 1, 3):
            xx = lax.rem(x + d, NX)
            send(remote(p4s.at[n, xx], p4.at[n, x], s4_send.at[n, d - 1], s4_recv.at[n, x],
                        to_ctx(ctx_at(z, y, xx))))
        p4[n, x] = p4s[n, x]

    def scan_end(n):
        for d in (1, 3, 2):
            xx = lax.rem(x + d, NX)
            arrived(p4.at[n, xx], s4_recv.at[n, xx])
        return [
            jnp.concatenate([p4[n, q, h] for q in range(NX)], axis=0) for h in range(nhead)
        ]

    def cols(h):
        return slice(h * HDIM, (h + 1) * HDIM)

    weights_y()
    local[0].wait()
    for k in range(AHEAD):
        h_issue(k)

    lg[...] = jnp.zeros_like(lg)
    lg[0:nhead, :] = logs[...]
    log_rows = lg[...]
    gate = jnp.sqrt(one_less_exp(2.0 * log_rows))
    lane = lax.broadcasted_iota(jnp.int32, log_rows.shape, 1)
    cumul = log_rows
    shift = 1
    while shift < tokens:
        cumul = cumul + jnp.where(lane >= shift, pltpu.roll(cumul, shift, 1), 0.0)
        shift *= 2
    total = cumul[:, tokens - 1 : tokens]
    tx[x] = jnp.broadcast_to(total, (8, HDIM))
    rows[0:8, :] = gate
    rows[8:16, :] = scale * jnp.exp(cumul)
    rows[16:24, :] = jnp.exp(total - cumul)
    rows[24:32, :] = cumul
    columns = jnp.transpose(rows[...])
    gate_c = [columns[:, h : h + 1] for h in range(nhead)]
    head_c = [columns[:, 8 + h : 9 + h] for h in range(nhead)]
    tail_c = [columns[:, 16 + h : 17 + h] for h in range(nhead)]
    cumul_c = [columns[:, 24 + h : 25 + h] for h in range(nhead)]

    states = []
    for h in range(nhead):
        scaled = (gate_c[h] * keys[:, cols(h)].astype(F32)).astype(BF16)
        sk[:, cols(h)] = scaled
        decayed = (tail_c[h] * scaled.astype(F32)).astype(BF16)
        states.append(mm_tn(decayed, values[:, cols(h)]))
    scan_x(0, states)
    weights_z()

    block = 128
    tri = lax.broadcasted_iota(jnp.int32, (block, block), 0) >= lax.broadcasted_iota(
        jnp.int32, (block, block), 1
    )
    for h in range(nhead):
        cumul_r = rows[24 + h : 25 + h, :]
        for t0 in range(0, tokens, block):
            t = slice(t0, t0 + block)
            for s0 in range(0, t0 + block, block):
                s = slice(s0, s0 + block)
                spread = cumul_c[h][t] - cumul_r[:, s]
                if s0 == t0:
                    decays = jnp.where(tri, jnp.exp(jnp.where(tri, spread, 0.0)) * scale, 0.0)
                else:
                    decays = jnp.exp(spread) * scale
                dots = mm_nt(d_out[t, cols(h)], values[s, cols(h)])
                dec[h, t, s] = decays
                wdv[h, t, s] = (decays * dots).astype(BF16)

    def intra_query(h, t0):
        t = slice(t0, t0 + block)
        return mm(wdv[h, t, 0 : t0 + block], sk[0 : t0 + block, cols(h)])

    scan_y(0)

    def h_product(k0, k1):
        for k in range(k0, k1):
            h_finish(k)
        t = slice(k0 * h_step, k1 * h_step)
        acc = jnp.zeros((t.stop - t.start, width), F32)
        for b in range(2 * NP):
            acc = acc + mm(hid[b, t, :], w[b * feats : (b + 1) * feats, :])
        query[t, :] = acc.astype(BF16)

    chunks = h_sib.shape[0]

    def h_chunk(k):
        h_forward(k)
        if k + AHEAD < chunks:
            h_issue(k + AHEAD)

    h_chunk(0)
    h_chunk(1)
    scan_z(0)
    h_product(0, 2)
    h_chunk(2)
    weights_x()
    h_chunk(3)
    h_product(2, 4)
    h_chunk(4)
    scan_back(0)
    h_chunk(5)
    h_product(4, 6)
    h_chunk(6)
    weights_forward()
    h_chunk(7)
    state_in = scan_end(0)
    h_product(6, 8)

    adjoints = []
    for h in range(nhead):
        decayed = (head_c[h] * query[:, cols(h)].astype(F32)).astype(BF16)
        adjoints.append(mm_tn(decayed, d_out[:, cols(h)]))
    scan_x(1, adjoints)

    for h in range(nhead):
        for t0 in range(0, tokens, block):
            t = slice(t0, t0 + block)
            carry = mm_nt(d_out[t, cols(h)], state_in[h])
            out = intra_query(h, t0) + head_c[h][t] * carry
            dqf[head, t, cols(h)] = out.astype(BF16)

    scan_y(1)
    q_chunks = q_sib.shape[0]
    for k in range(q_chunks):
        q_issue(k)

    for h in range(nhead):
        for s0 in range(0, tokens, block):
            s = slice(s0, s0 + block)
            later = slice(s0, tokens)
            scores = mm_nt(query[later, cols(h)], sk[s, cols(h)])
            weight = (dec[h, later, s] * scores).astype(BF16)
            sums[0, s, cols(h)] = mm_tn(wdv[h, later, s], query[later, cols(h)])
            sums[1, s, cols(h)] = mm_tn(weight, d_out[later, cols(h)])

    scan_z(1)
    q_forward(0)
    weights_end()
    q_forward(1)
    scan_back(1)
    q_forward(2)
    q_forward(3)
    adjoint_in = scan_end(1)
    for h in range(nhead):
        carry_keys = mm_nt(values[:, cols(h)], adjoint_in[h])
        carry_values = mm(sk[:, cols(h)], adjoint_in[h])
        d_scaled = sums[0, :, cols(h)] + tail_c[h] * carry_keys
        dk_ref[:, cols(h)] = (gate_c[h] * d_scaled).astype(BF16)
        dv_ref[:, cols(h)] = (sums[1, :, cols(h)] + tail_c[h] * carry_values).astype(BF16)
    for k in range(q_chunks):
        q_finish(k)
        t = slice(k * q_step, (k + 1) * q_step)
        acc = jnp.zeros((q_step, feats), F32)
        for b in range(2 * NP):
            acc = acc + mm_nt(dqf[b, t, :], wr[b])
        dh_ref[t, :] = acc.astype(BF16)

    for cond, copy in pending:
        if cond is None:
            copy.wait_send()
        else:
            @pl.when(cond)
            def _(copy=copy):
                copy().wait_send()


def body(hidden, w_query, keys, values, d_out, log_decay):
    tokens, feats = hidden.shape
    width = w_query.shape[1]
    nhead = width // HDIM
    groups = 2 * NP
    h_chunks, q_chunks = 8, 4
    dma = pltpu.SemaphoreType.DMA
    vmem = pltpu.VMEM
    scratch = [
        vmem((groups, tokens, feats), BF16),
        vmem(w_query.shape, BF16),
        vmem((groups, feats, width), BF16),
        vmem((groups, tokens, width), BF16),
        vmem((tokens, width), BF16),
        vmem((tokens, width), BF16),
        vmem((8, tokens), F32),
        vmem((128, tokens), F32),
        vmem((nhead, tokens, tokens), F32),
        vmem((nhead, tokens, tokens), BF16),
        vmem((2, NX, nhead, QUARTER, HDIM), BF16),
        vmem((2, NX, nhead, QUARTER, HDIM), BF16),
        vmem((2, NY, nhead, QUARTER, HDIM), BF16),
        vmem((2, NZ, nhead, QUARTER, HDIM), BF16),
        vmem((2, NX, nhead, QUARTER, HDIM), BF16),
        vmem((2, NX, nhead, QUARTER, HDIM), BF16),
        vmem((NX, 8, HDIM), F32),
        vmem((NY, 8, HDIM), F32),
        vmem((NZ, 8, HDIM), F32),
        vmem((2, tokens, width), F32),
        dma((2,)),
    ]
    for chunks in (h_chunks, q_chunks):
        scratch += [dma((4, chunks)), dma((chunks,)), dma((3, chunks)), dma((chunks,)),
                    dma((groups, chunks))]
    scratch += [dma((groups - 1,)), dma((groups,)), dma((NZ - 1,)), dma((NZ,)),
                dma((2,)), dma((2,)), dma((2,)), dma((2,))]
    scratch += [dma((2, NX - 1)), dma((2, NX)), dma((2,)), dma((2, NY)),
                dma((2, NZ - 1)), dma((2, NZ)), dma((2, NX - 1)), dma((2, NX))]
    scratch += [dma((NX - 1,)), dma((NX,)), dma((1,)), dma((NY,)), dma((NZ - 1,)), dma((NZ,))]
    in_vmem = pl.BlockSpec(memory_space=pltpu.VMEM)
    anywhere = pl.BlockSpec(memory_space=pl.ANY)
    return pl.pallas_call(
        kernel,
        out_shape=(
            jax.ShapeDtypeStruct((tokens, feats), BF16),
            jax.ShapeDtypeStruct((tokens, width), BF16),
            jax.ShapeDtypeStruct((tokens, width), BF16),
        ),
        in_specs=[anywhere, anywhere, in_vmem, in_vmem, in_vmem, in_vmem],
        out_specs=(in_vmem, in_vmem, in_vmem),
        scratch_shapes=scratch,
        compiler_params=pltpu.CompilerParams(
            collective_id=0, has_side_effects=True, vmem_limit_bytes=56 * 1024 * 1024
        ),
    )(hidden, w_query, keys, values, d_out, log_decay.T)


def solution(mesh):
    return jax.shard_map(
        body,
        mesh=mesh,
        in_specs=(
            P("ctx", "head"),
            P(None, "head"),
            P("ctx", "head"),
            P("ctx", "head"),
            P("ctx", "head"),
            P("ctx", "head"),
        ),
        out_specs=(P("ctx", "head"), P("ctx", "head"), P("ctx", "head")),
        check_vma=False,
    )
```

```python
import functools

import jax
import jax.numpy as jnp
from jax import lax
from jax.experimental import pallas as pl
from jax.experimental.pallas import tpu as pltpu
from jax.sharding import PartitionSpec as P

MESH = pl.DeviceIdType.MESH
F32 = jnp.float32
BF16 = jnp.bfloat16
HDIM = 128
NX, NY, NZ = 4, 2, 8
NP = 4
QUARTER = HDIM // NX
OFFSETS = (2, -2, 1, -1)
AHEAD = 3


def mm(a, b):
    return lax.dot_general(a, b, (((1,), (0,)), ((), ())), preferred_element_type=F32)


def mm_nt(a, b):
    return lax.dot_general(a, b, (((1,), (1,)), ((), ())), preferred_element_type=F32)


def mm_tn(a, b):
    return lax.dot_general(a, b, (((0,), (0,)), ((), ())), preferred_element_type=F32)


def one_less_exp(x):
    series = jnp.full_like(x, 1.0)
    for n in range(9, 1, -1):
        series = 1.0 + x * (1.0 / n) * series
    return jnp.where(x > -0.5, -x * series, 1.0 - jnp.exp(x))


def kernel(
    hidden, w_hbm, keys_hbm, values_hbm, d_out_hbm, logs_hbm,
    dh_hbm, dk_hbm, dv_hbm,
    logs, keys, values, d_out, dh_ref, dk_ref, dv_ref,
    hid, w, wr, dqf, query, sk, lg, rows, dec, wdv,
    loc, p1, p2, p3, p4s, p4, tx, by, bz, sums,
    in_sem, out_sem,
    h_send, h_recv, h_near,
    q_send, q_recv, q_near,
    wy_send, wy_recv, wz_send, wz_recv, wx_send, wx_recv, wf_send, wf_recv,
    s_send, s_recv, t_send, t_recv,
):
    scale = HDIM ** (-0.5)
    tokens = hidden.shape[0]
    feats = hidden.shape[1]
    width = w_hbm.shape[1]
    nhead = width // HDIM
    ctx, head = lax.axis_index("ctx"), lax.axis_index("head")
    x = lax.rem(ctx, NX)
    y = lax.rem(lax.div(ctx, NX), NY)
    z = lax.div(ctx, NX * NY)
    chip, core = lax.div(head, 2), lax.rem(head, 2)
    sib = 2 * chip + 1 - core

    def ctx_at(zz, yy, xx):
        return (zz * NY + yy) * NX + xx

    def to_head(other):
        return {"head": other}

    def to_ctx(other):
        return {"ctx": other}

    def remote(src, dst, send, recv, device):
        return pltpu.make_async_remote_copy(
            src_ref=src, dst_ref=dst, send_sem=send, recv_sem=recv,
            device_id=device, device_id_type=MESH,
        )

    def arrived(dst, sem):
        remote(dst, dst, sem, sem, to_head(sib)).wait_recv()

    pending = []

    def sent(src, sem, cond=None):
        pending.append((cond, src, sem))

    barrier = pltpu.get_barrier_semaphore()
    partners = [to_head(lax.rem(head + d, 2 * NP)) for d in range(1, 2 * NP)]
    partners += [to_ctx(ctx_at(z, y, lax.rem(x + d, NX))) for d in range(1, NX)]
    partners += [to_ctx(ctx_at(z, 1 - y, x))]
    partners += [to_ctx(ctx_at(lax.rem(z + d, NZ), y, x)) for d in range(1, NZ)]
    for partner in partners:
        pl.semaphore_signal(barrier, inc=1, device_id=partner, device_id_type=MESH)

    local = [
        pltpu.make_async_copy(src, dst, in_sem.at[i])
        for i, (src, dst) in enumerate((
            (hidden, hid.at[head]), (w_hbm, w), (keys_hbm, keys),
            (values_hbm, values), (d_out_hbm, d_out), (logs_hbm, logs),
        ))
    ]
    lg[...] = jnp.zeros_like(lg)
    for i in (5, 2, 3, 0, 1, 4):
        local[i].start()

    def drain():
        for cond, src, sem in pending:
            copy = remote(src, src, sem, sem, to_head(sib))
            if cond is None:
                copy.wait_send()
            else:
                pl.when(cond)(copy.wait_send)

    part = feats // (NX * NZ)
    slot = pl.multiple_of((x * NZ + z) * part, part)

    def weights_y():
        local[1].wait()
        mine = w.at[pl.ds(pl.multiple_of(head * feats + slot, part), part), :]
        for d in range(1, 2 * NP):
            other = lax.rem(head + d, 2 * NP)
            remote(
                w.at[pl.ds(pl.multiple_of(other * feats + slot, part), part), :],
                wr.at[head, pl.ds(slot, part), :],
                wy_send.at[0], wy_recv.at[0], to_head(other),
            ).start()
        sent(wr.at[pl.ds(0, 2 * NP - 1), pl.ds(0, part), :], wy_send.at[0])
        wr[head, pl.ds(slot, part), :] = mine[...]

    def weights_z():
        arrived(wr.at[pl.ds(0, 2 * NP - 1), pl.ds(0, part), :], wy_recv.at[0])
        mine = wr.at[:, pl.ds(slot, part), :]
        for d in (4, 3, 5, 2, 6, 1, 7):
            remote(mine, mine, wz_send.at[0], wz_recv.at[0],
                   to_ctx(ctx_at(lax.rem(z + d, NZ), y, x))).start()
        sent(wr.at[:, pl.ds(0, (NZ - 1) * part), :], wz_send.at[0])

    line = part * NZ
    right, left = lax.rem(x + 1, NX), lax.rem(x + NX - 1, NX)
    across = lax.rem(x + 2, NX)

    def line_of(xx):
        return pl.ds(pl.multiple_of(xx * line, line), line)

    def send(src, send_sem, recv_sem, device):
        remote(src, src, send_sem, recv_sem, device).start()
        sent(src, send_sem)

    def weights_x():
        arrived(wr.at[:, pl.ds(0, (NZ - 1) * part), :], wz_recv.at[0])
        mine = wr.at[:, line_of(x), :]
        send(mine, wx_send.at[0], wx_recv.at[0], to_ctx(ctx_at(z, y, right)))
        send(mine, wx_send.at[1], wx_recv.at[1], to_ctx(ctx_at(z, y, left)))

    def weights_forward():
        arrived(wr.at[:, line_of(left), :], wx_recv.at[0])
        half = wr.at[pl.ds(0, NP), line_of(left), :]
        send(half, wf_send.at[0], wf_recv.at[0], to_ctx(ctx_at(z, y, right)))
        arrived(wr.at[:, line_of(right), :], wx_recv.at[1])
        half = wr.at[pl.ds(NP, NP), line_of(right), :]
        send(half, wf_send.at[1], wf_recv.at[1], to_ctx(ctx_at(z, y, left)))

    def weights_end():
        arrived(wr.at[pl.ds(0, NP), line_of(across), :], wf_recv.at[0])
        arrived(wr.at[pl.ds(NP, NP), line_of(across), :], wf_recv.at[1])

    def gather(buf, s_send, s_recv, s_near):
        chunks, groups = s_recv.shape[1], s_near.shape[0]
        step = tokens // chunks
        per = chunks // groups
        targets = []
        for d in OFFSETS:
            other = chip + d
            targets.append((other, jnp.logical_and(other >= 0, other < NP)))
        relays = jnp.logical_and(chip >= 1, chip <= 2)
        end = jnp.where(chip == 2, 3, 0)

        def piece(block, k):
            return buf.at[block, pl.ds(k * step, step), :]

        def issue(k):
            mine = piece(head, k)
            for i, (other, ok) in enumerate(targets):
                pl.when(ok)(remote(mine, mine, s_send.at[i], s_recv.at[chip, k],
                                   to_head(2 * other + core)).start)
            remote(mine, mine, s_send.at[4], s_near.at[k // per], to_head(sib)).start()

        def forward(k):
            for i, d in enumerate((2, 1, 3)):
                source = lax.rem(chip + d, NP)
                got = piece(2 * source + core, k)
                recv = s_recv.at[source, k]
                arrived(got, recv)
                if d == 2:
                    pl.when(relays)(remote(got, got, s_send.at[5], recv,
                                           to_head(2 * end + core)).start)
                remote(got, got, s_send.at[6 + i], s_near.at[k // per], to_head(sib)).start()

        def finish(group):
            arrived(buf.at[pl.ds(0, NP), pl.ds(group * per * step, per * step), :],
                    s_near.at[group])

        def close():
            for i, (_, ok) in enumerate(targets):
                sent(buf.at[head], s_send.at[i], ok)
            sent(buf.at[head], s_send.at[4])
            sent(buf.at[head], s_send.at[5], relays)
            for i in range(3):
                sent(buf.at[head], s_send.at[6 + i])

        return issue, forward, finish, close

    h_issue, h_forward, h_finish, h_close = gather(hid, h_send, h_recv, h_near)
    q_issue, q_forward, q_finish, q_close = gather(dqf, q_send, q_recv, q_near)
    h_step = tokens // h_recv.shape[1]
    q_step = tokens // q_recv.shape[1]

    def line_fold(parts, gains, reverse, start):
        outs = [None] * len(parts)
        acc = start
        order = range(len(parts))
        for i in reversed(order) if reverse else order:
            outs[i] = acc
            acc = [gains[i][h] * acc[h] + parts[i][h] for h in range(nhead)]
        return outs, acc

    def zeros():
        return [jnp.zeros((QUARTER, HDIM), F32) for _ in range(nhead)]

    def gains_of(ref, count):
        return [[jnp.exp(ref[i][h : h + 1, :]) for h in range(nhead)] for i in range(count)]

    def parts_of(ref, n, count):
        return [[ref[n, i, h].astype(F32) for h in range(nhead)] for i in range(count)]

    def scan_x(n, states):
        for q in range(NX):
            for h in range(nhead):
                loc[n, q, h] = states[h][q * QUARTER : (q + 1) * QUARTER].astype(BF16)
        for d in (2, 1, 3):
            xx = lax.rem(x + d, NX)
            device = to_ctx(ctx_at(z, y, xx))
            remote(loc.at[n, xx], p1.at[n, x], s_send.at[n, 0], s_recv.at[n, 0], device).start()
            if n == 0:
                remote(tx.at[x], tx.at[x], t_send.at[0], t_recv.at[0], device).start()
        sent(loc.at[n, pl.ds(0, NX - 1)], s_send.at[n, 0])
        if n == 0:
            sent(tx.at[pl.ds(0, NX - 1)], t_send.at[0])
        p1[n, x] = loc[n, x]

    def scan_y(n):
        arrived(p1.at[n, pl.ds(0, NX - 1)], s_recv.at[n, 0])
        if n == 0:
            arrived(tx.at[pl.ds(0, NX - 1)], t_recv.at[0])
            by[y] = tx[0] + tx[1] + tx[2] + tx[3]
        _, total = line_fold(parts_of(p1, n, NX), gains_of(tx, NX), n == 1, zeros())
        for h in range(nhead):
            p2[n, y, h] = total[h].astype(BF16)
        device = to_ctx(ctx_at(z, 1 - y, x))
        send(p2.at[n, y], s_send.at[n, 1], s_recv.at[n, 1], device)
        if n == 0:
            send(by.at[y], t_send.at[1], t_recv.at[1], device)

    def scan_z(n):
        arrived(p2.at[n, 1 - y], s_recv.at[n, 1])
        if n == 0:
            arrived(by.at[1 - y], t_recv.at[1])
            bz[z] = by[0] + by[1]
        _, total = line_fold(parts_of(p2, n, NY), gains_of(by, NY), n == 1, zeros())
        for h in range(nhead):
            p3[n, z, h] = total[h].astype(BF16)
        for d in (4, 3, 5, 2, 6, 1, 7):
            device = to_ctx(ctx_at(lax.rem(z + d, NZ), y, x))
            remote(p3.at[n, z], p3.at[n, z], s_send.at[n, 2], s_recv.at[n, 2], device).start()
            if n == 0:
                remote(bz.at[z], bz.at[z], t_send.at[2], t_recv.at[2], device).start()
        sent(p3.at[n, pl.ds(0, NZ - 1)], s_send.at[n, 2])
        if n == 0:
            sent(bz.at[pl.ds(0, NZ - 1)], t_send.at[2])

    def scan_back(n):
        arrived(p3.at[n, pl.ds(0, NZ - 1)], s_recv.at[n, 2])
        if n == 0:
            arrived(bz.at[pl.ds(0, NZ - 1)], t_recv.at[2])
        reverse = n == 1
        gains = gains_of(bz, NZ)
        parts = parts_of(p3, n, NZ)
        acc = zeros()
        for i in reversed(range(NZ)) if reverse else range(NZ):
            use = z < i if reverse else z > i
            keep = jnp.where(use, 1.0, 0.0)
            acc = [
                acc[h] * (1.0 - keep + keep * gains[i][h]) + keep * parts[i][h]
                for h in range(nhead)
            ]
        outs, _ = line_fold(parts_of(p2, n, NY), gains_of(by, NY), reverse, acc)
        first = jnp.where(y == 0, 1.0, 0.0)
        acc = [first * outs[0][h] + (1.0 - first) * outs[1][h] for h in range(nhead)]
        outs, _ = line_fold(parts_of(p1, n, NX), gains_of(tx, NX), reverse, acc)
        for i in range(NX):
            for h in range(nhead):
                p4s[n, i, h] = outs[i][h].astype(BF16)
        for d in (2, 1, 3):
            xx = lax.rem(x + d, NX)
            remote(p4s.at[n, xx], p4.at[n, x], s_send.at[n, 3], s_recv.at[n, 3],
                   to_ctx(ctx_at(z, y, xx))).start()
        sent(p4s.at[n, pl.ds(0, NX - 1)], s_send.at[n, 3])
        p4[n, x] = p4s[n, x]

    def scan_end(n):
        arrived(p4.at[n, pl.ds(0, NX - 1)], s_recv.at[n, 3])
        return [
            jnp.concatenate([p4[n, q, h] for q in range(NX)], axis=0) for h in range(nhead)
        ]

    def cols(h):
        return slice(h * HDIM, (h + 1) * HDIM)

    local[5].wait()
    lg[0:nhead, :] = logs[...]
    log_rows = lg[...]
    gate = jnp.sqrt(one_less_exp(2.0 * log_rows))
    lane = lax.broadcasted_iota(jnp.int32, log_rows.shape, 1)
    cumul = log_rows
    shift = 1
    while shift < tokens:
        cumul = cumul + jnp.where(lane >= shift, pltpu.roll(cumul, shift, 1), 0.0)
        shift *= 2
    total = cumul[:, tokens - 1 : tokens]
    tx[x] = jnp.broadcast_to(total, (8, HDIM))
    rows[0:8, :] = gate
    rows[8:16, :] = scale * jnp.exp(cumul)
    rows[16:24, :] = jnp.exp(total - cumul)
    rows[24:32, :] = cumul
    columns = jnp.transpose(rows[...])
    gate_c = [columns[:, h : h + 1] for h in range(nhead)]
    head_c = [columns[:, 8 + h : 9 + h] for h in range(nhead)]
    tail_c = [columns[:, 16 + h : 17 + h] for h in range(nhead)]
    cumul_c = [columns[:, 24 + h : 25 + h] for h in range(nhead)]

    local[2].wait()
    local[3].wait()
    states = []
    for h in range(nhead):
        scaled = (gate_c[h] * keys[:, cols(h)].astype(F32)).astype(BF16)
        sk[:, cols(h)] = scaled
        decayed = (tail_c[h] * scaled.astype(F32)).astype(BF16)
        states.append(mm_tn(decayed, values[:, cols(h)]))

    pl.semaphore_wait(barrier, len(partners))
    weights_y()
    local[0].wait()
    for k in range(AHEAD):
        h_issue(k)
    scan_x(0, states)

    local[4].wait()
    block = 128
    tri = lax.broadcasted_iota(jnp.int32, (block, block), 0) >= lax.broadcasted_iota(
        jnp.int32, (block, block), 1
    )
    for h in range(nhead):
        cumul_r = rows[24 + h : 25 + h, :]
        for t0 in range(0, tokens, block):
            t = slice(t0, t0 + block)
            for s0 in range(0, t0 + block, block):
                s = slice(s0, s0 + block)
                spread = cumul_c[h][t] - cumul_r[:, s]
                if s0 == t0:
                    decays = jnp.where(tri, jnp.exp(jnp.where(tri, spread, 0.0)) * scale, 0.0)
                else:
                    decays = jnp.exp(spread) * scale
                dots = mm_nt(d_out[t, cols(h)], values[s, cols(h)])
                dec[h, t, s] = decays
                wdv[h, t, s] = (decays * dots).astype(BF16)

    def intra_query(h, t0):
        t = slice(t0, t0 + block)
        return mm(wdv[h, t, 0 : t0 + block], sk[0 : t0 + block, cols(h)])

    weights_z()
    scan_y(0)

    def h_product(k0, k1):
        h_finish(k0 // 2)
        t = slice(k0 * h_step, k1 * h_step)
        acc = jnp.zeros((t.stop - t.start, width), F32)
        for b in range(2 * NP):
            acc = acc + mm(hid[b, t, :], w[b * feats : (b + 1) * feats, :])
        query[t, :] = acc.astype(BF16)

    chunks = h_recv.shape[1]

    def h_chunk(k):
        h_forward(k)
        if k + AHEAD < chunks:
            h_issue(k + AHEAD)

    h_chunk(0)
    h_chunk(1)
    scan_z(0)
    h_product(0, 2)
    h_chunk(2)
    weights_x()
    h_chunk(3)
    scan_back(0)
    h_product(2, 4)
    h_chunk(4)
    h_chunk(5)
    h_product(4, 6)

    state_in = scan_end(0)
    for h in range(nhead):
        for t0 in range(0, tokens, block):
            t = slice(t0, t0 + block)
            carry = mm_nt(d_out[t, cols(h)], state_in[h])
            out = intra_query(h, t0) + head_c[h][t] * carry
            dqf[head, t, cols(h)] = out.astype(BF16)

    h_chunk(6)
    h_chunk(7)
    q_issue(0)
    h_product(6, 8)

    adjoints = []
    for h in range(nhead):
        decayed = (head_c[h] * query[:, cols(h)].astype(F32)).astype(BF16)
        adjoints.append(mm_tn(decayed, d_out[:, cols(h)]))
    scan_x(1, adjoints)
    q_chunks = q_recv.shape[1]
    q_issue(1)

    for h in range(nhead):
        for s0 in range(0, tokens, block):
            s = slice(s0, s0 + block)
            later = slice(s0, tokens)
            scores = mm_nt(query[later, cols(h)], sk[s, cols(h)])
            weight = (dec[h, later, s] * scores).astype(BF16)
            sums[0, s, cols(h)] = mm_tn(wdv[h, later, s], query[later, cols(h)])
            sums[1, s, cols(h)] = mm_tn(weight, d_out[later, cols(h)])

    outs = []

    def out_copy(src, dst):
        copy = pltpu.make_async_copy(src, dst, out_sem.at[len(outs)])
        copy.start()
        outs.append(copy)

    def q_product(k):
        q_finish(k)
        t = slice(k * q_step, (k + 1) * q_step)
        acc = jnp.zeros((q_step, feats), F32)
        for b in range(2 * NP):
            acc = acc + mm_nt(dqf[b, t, :], wr[b])
        dh_ref[t, :] = acc.astype(BF16)
        out_copy(dh_ref.at[t, :], dh_hbm.at[t, :])

    scan_y(1)
    for k in range(2, q_chunks):
        q_issue(k)
    weights_forward()
    q_forward(0)
    scan_z(1)
    q_forward(1)
    weights_end()
    q_product(0)
    q_forward(2)
    scan_back(1)
    q_product(1)
    q_forward(3)
    adjoint_in = scan_end(1)
    for h in range(nhead):
        carry_keys = mm_nt(values[:, cols(h)], adjoint_in[h])
        carry_values = mm(sk[:, cols(h)], adjoint_in[h])
        d_scaled = sums[0, :, cols(h)] + tail_c[h] * carry_keys
        dk_ref[:, cols(h)] = (gate_c[h] * d_scaled).astype(BF16)
        dv_ref[:, cols(h)] = (sums[1, :, cols(h)] + tail_c[h] * carry_values).astype(BF16)
    out_copy(dk_ref, dk_hbm)
    out_copy(dv_ref, dv_hbm)
    q_product(2)
    q_product(3)
    h_close()
    q_close()
    drain()
    for copy in outs:
        copy.wait()


def finish(*refs):
    n = 3
    sems = refs[2 * n]
    copies = [pltpu.make_async_copy(refs[i], refs[n + i], sems.at[i]) for i in range(n)]
    for copy in copies:
        copy.start()
    for copy in copies:
        copy.wait()


def body(hidden, w_query, keys, values, d_out, log_decay):
    tokens, feats = hidden.shape
    width = w_query.shape[1]
    nhead = width // HDIM
    groups = 2 * NP
    h_chunks, q_chunks = 8, 4
    dma = pltpu.SemaphoreType.DMA
    vmem = pltpu.VMEM
    scratch = [
        vmem((nhead, tokens), F32),
        vmem((tokens, width), BF16),
        vmem((tokens, width), BF16),
        vmem((tokens, width), BF16),
        vmem((tokens, feats), BF16),
        vmem((tokens, width), BF16),
        vmem((tokens, width), BF16),
        vmem((groups, tokens, feats), BF16),
        vmem(w_query.shape, BF16),
        vmem((groups, feats, width), BF16),
        vmem((groups, tokens, width), BF16),
        vmem((tokens, width), BF16),
        vmem((tokens, width), BF16),
        vmem((8, tokens), F32),
        vmem((128, tokens), F32),
        vmem((nhead, tokens, tokens), F32),
        vmem((nhead, tokens, tokens), BF16),
        vmem((2, NX, nhead, QUARTER, HDIM), BF16),
        vmem((2, NX, nhead, QUARTER, HDIM), BF16),
        vmem((2, NY, nhead, QUARTER, HDIM), BF16),
        vmem((2, NZ, nhead, QUARTER, HDIM), BF16),
        vmem((2, NX, nhead, QUARTER, HDIM), BF16),
        vmem((2, NX, nhead, QUARTER, HDIM), BF16),
        vmem((NX, 8, HDIM), F32),
        vmem((NY, 8, HDIM), F32),
        vmem((NZ, 8, HDIM), F32),
        vmem((2, tokens, width), F32),
        dma((6,)),
        dma((q_chunks + 2,)),
    ]
    for chunks in (h_chunks, q_chunks):
        scratch += [dma((9,)), dma((NP, chunks)), dma((4,))]
    scratch += [dma((1,))] * 4 + [dma((2,))] * 4
    scratch += [dma((2, 4)), dma((2, 4)), dma((3,)), dma((3,))]
    anywhere = pl.BlockSpec(memory_space=pl.ANY)
    shapes = (
        jax.ShapeDtypeStruct((tokens, feats), BF16),
        jax.ShapeDtypeStruct((tokens, width), BF16),
        jax.ShapeDtypeStruct((tokens, width), BF16),
    )
    results = pl.pallas_call(
        kernel,
        out_shape=shapes,
        in_specs=[pl.BlockSpec(memory_space=pltpu.HBM)] * 6,
        out_specs=(anywhere,) * 3,
        scratch_shapes=scratch,
        compiler_params=pltpu.CompilerParams(
            collective_id=0, has_side_effects=True, vmem_limit_bytes=32 * 1024 * 1024
        ),
    )(*(pltpu.with_memory_space_constraint(a, pltpu.HBM) for a in (hidden, w_query, keys, values, d_out, log_decay.T)))
    return pl.pallas_call(
        finish,
        out_shape=shapes,
        in_specs=[anywhere] * 3,
        out_specs=(anywhere,) * 3,
        scratch_shapes=[dma((3,))],
        compiler_params=pltpu.CompilerParams(vmem_limit_bytes=4 * 1024 * 1024),
    )(*results)


def solution(mesh):
    return jax.shard_map(
        body,
        mesh=mesh,
        in_specs=(
            P("ctx", "head"),
            P(None, "head"),
            P("ctx", "head"),
            P("ctx", "head"),
            P("ctx", "head"),
            P("ctx", "head"),
        ),
        out_specs=(P("ctx", "head"), P("ctx", "head"), P("ctx", "head")),
        check_vma=False,
    )
```

```python
import functools

import jax
import jax.numpy as jnp
from jax import lax
from jax.experimental import pallas as pl
from jax.experimental.pallas import tpu as pltpu
from jax.sharding import PartitionSpec as P

MESH = pl.DeviceIdType.MESH
F32 = jnp.float32
BF16 = jnp.bfloat16
HDIM = 128
NX, NY, NZ = 4, 2, 8
NP = 4
QUARTER = HDIM // NX
OFFSETS = (2, -2, 1, -1)
AHEAD = (4, 2)


def mm(a, b):
    return lax.dot_general(a, b, (((1,), (0,)), ((), ())), preferred_element_type=F32)


def mm_nt(a, b):
    return lax.dot_general(a, b, (((1,), (1,)), ((), ())), preferred_element_type=F32)


def mm_tn(a, b):
    return lax.dot_general(a, b, (((0,), (0,)), ((), ())), preferred_element_type=F32)


def one_less_exp(x):
    series = jnp.full_like(x, 1.0)
    for n in range(9, 1, -1):
        series = 1.0 + x * (1.0 / n) * series
    return jnp.where(x > -0.5, -x * series, 1.0 - jnp.exp(x))


def kernel(
    hidden, w_hbm, keys_hbm, values_hbm, d_out_hbm, logs_hbm,
    dh_hbm, dk_hbm, dv_hbm,
    logs, keys, values, d_out, dh_ref, dk_ref, dv_ref,
    hid, w, wr, dqf, query, sk, lg, rows, dec, wdv,
    loc, p1, p2, p3, p4s, p4, tx, by, bz, sums,
    in_sem, out_sem,
    h_send, h_recv, h_near,
    q_send, q_recv, q_near,
    wy_send, wy_recv, wz_send, wz_recv, wx_send, wx_recv, wf_send, wf_recv,
    s_send, s_recv, t_send, t_recv,
):
    scale = HDIM ** (-0.5)
    tokens = hidden.shape[0]
    feats = hidden.shape[1]
    width = w_hbm.shape[1]
    nhead = width // HDIM
    ctx, head = lax.axis_index("ctx"), lax.axis_index("head")
    x = lax.rem(ctx, NX)
    y = lax.rem(lax.div(ctx, NX), NY)
    z = lax.div(ctx, NX * NY)
    chip, core = lax.div(head, 2), lax.rem(head, 2)
    sib = 2 * chip + 1 - core

    def ctx_at(zz, yy, xx):
        return (zz * NY + yy) * NX + xx

    def to_head(other):
        return {"head": other}

    def to_ctx(other):
        return {"ctx": other}

    def remote(src, dst, send, recv, device):
        return pltpu.make_async_remote_copy(
            src_ref=src, dst_ref=dst, send_sem=send, recv_sem=recv,
            device_id=device, device_id_type=MESH,
        )

    def arrived(dst, sem):
        remote(dst, dst, sem, sem, to_head(sib)).wait_recv()

    pending = []

    def sent(src, sem, cond=None):
        pending.append((cond, src, sem))

    barrier = pltpu.get_barrier_semaphore()
    partners = [to_head(lax.rem(head + d, 2 * NP)) for d in range(1, 2 * NP)]
    partners += [to_ctx(ctx_at(z, y, lax.rem(x + d, NX))) for d in range(1, NX)]
    partners += [to_ctx(ctx_at(z, 1 - y, x))]
    partners += [to_ctx(ctx_at(lax.rem(z + d, NZ), y, x)) for d in range(1, NZ)]
    for partner in partners:
        pl.semaphore_signal(barrier, inc=1, device_id=partner, device_id_type=MESH)

    local = [
        pltpu.make_async_copy(src, dst, in_sem.at[i])
        for i, (src, dst) in enumerate((
            (hidden, hid.at[head]), (w_hbm, w), (keys_hbm, keys),
            (values_hbm, values), (d_out_hbm, d_out), (logs_hbm, logs),
        ))
    ]
    lg[...] = jnp.zeros_like(lg)
    for i in (5, 2, 3, 0, 1, 4):
        local[i].start()

    def drain():
        for cond, src, sem in pending:
            copy = remote(src, src, sem, sem, to_head(sib))
            if cond is None:
                copy.wait_send()
            else:
                pl.when(cond)(copy.wait_send)

    part = feats // (NX * NZ)
    slot = pl.multiple_of((x * NZ + z) * part, part)

    def weights_y():
        local[1].wait()
        mine = w.at[pl.ds(pl.multiple_of(head * feats + slot, part), part), :]
        for d in range(1, 2 * NP):
            other = lax.rem(head + d, 2 * NP)
            remote(
                w.at[pl.ds(pl.multiple_of(other * feats + slot, part), part), :],
                wr.at[head, pl.ds(slot, part), :],
                wy_send.at[0], wy_recv.at[0], to_head(other),
            ).start()
        sent(wr.at[pl.ds(0, 2 * NP - 1), pl.ds(0, part), :], wy_send.at[0])
        wr[head, pl.ds(slot, part), :] = mine[...]

    def weights_z():
        arrived(wr.at[pl.ds(0, 2 * NP - 1), pl.ds(0, part), :], wy_recv.at[0])
        mine = wr.at[:, pl.ds(slot, part), :]
        for d in (4, 3, 5, 2, 6, 1, 7):
            remote(mine, mine, wz_send.at[0], wz_recv.at[0],
                   to_ctx(ctx_at(lax.rem(z + d, NZ), y, x))).start()
        sent(wr.at[:, pl.ds(0, (NZ - 1) * part), :], wz_send.at[0])

    line = part * NZ
    right, left = lax.rem(x + 1, NX), lax.rem(x + NX - 1, NX)
    across = lax.rem(x + 2, NX)

    def line_of(xx):
        return pl.ds(pl.multiple_of(xx * line, line), line)

    def send(src, send_sem, recv_sem, device):
        remote(src, src, send_sem, recv_sem, device).start()
        sent(src, send_sem)

    def weights_x():
        arrived(wr.at[:, pl.ds(0, (NZ - 1) * part), :], wz_recv.at[0])
        mine = wr.at[:, line_of(x), :]
        send(mine, wx_send.at[0], wx_recv.at[0], to_ctx(ctx_at(z, y, right)))
        send(mine, wx_send.at[1], wx_recv.at[1], to_ctx(ctx_at(z, y, left)))

    def weights_forward():
        arrived(wr.at[:, line_of(left), :], wx_recv.at[0])
        half = wr.at[pl.ds(0, NP), line_of(left), :]
        send(half, wf_send.at[0], wf_recv.at[0], to_ctx(ctx_at(z, y, right)))
        arrived(wr.at[:, line_of(right), :], wx_recv.at[1])
        half = wr.at[pl.ds(NP, NP), line_of(right), :]
        send(half, wf_send.at[1], wf_recv.at[1], to_ctx(ctx_at(z, y, left)))

    def weights_end():
        arrived(wr.at[pl.ds(0, NP), line_of(across), :], wf_recv.at[0])
        arrived(wr.at[pl.ds(NP, NP), line_of(across), :], wf_recv.at[1])

    def gather(buf, s_send, s_recv, s_near):
        chunks, groups = s_recv.shape[1], s_near.shape[0]
        step = tokens // chunks
        per = chunks // groups
        targets = []
        for d in OFFSETS:
            other = chip + d
            targets.append((other, jnp.logical_and(other >= 0, other < NP)))
        relays = jnp.logical_and(chip >= 1, chip <= 2)
        end = jnp.where(chip == 2, 3, 0)

        def piece(block, k):
            return buf.at[block, pl.ds(k * step, step), :]

        def issue(k):
            mine = piece(head, k)
            for i, (other, ok) in enumerate(targets):
                pl.when(ok)(remote(mine, mine, s_send.at[i], s_recv.at[chip, k],
                                   to_head(2 * other + core)).start)
            remote(mine, mine, s_send.at[4], s_near.at[k // per], to_head(sib)).start()

        def forward(k):
            for i, d in enumerate((2, 1, 3)):
                source = lax.rem(chip + d, NP)
                got = piece(2 * source + core, k)
                recv = s_recv.at[source, k]
                arrived(got, recv)
                if d == 2:
                    pl.when(relays)(remote(got, got, s_send.at[5], recv,
                                           to_head(2 * end + core)).start)
                remote(got, got, s_send.at[6 + i], s_near.at[k // per], to_head(sib)).start()

        def finish(group):
            arrived(buf.at[pl.ds(0, NP), pl.ds(group * per * step, per * step), :],
                    s_near.at[group])

        def close():
            for i, (_, ok) in enumerate(targets):
                sent(buf.at[head], s_send.at[i], ok)
            sent(buf.at[head], s_send.at[4])
            sent(buf.at[head], s_send.at[5], relays)
            for i in range(3):
                sent(buf.at[head], s_send.at[6 + i])

        return issue, forward, finish, close

    h_issue, h_forward, h_finish, h_close = gather(hid, h_send, h_recv, h_near)
    q_issue, q_forward, q_finish, q_close = gather(dqf, q_send, q_recv, q_near)
    h_step = tokens // h_recv.shape[1]
    q_step = tokens // q_recv.shape[1]

    def line_fold(parts, gains, reverse, start):
        outs = [None] * len(parts)
        acc = start
        order = range(len(parts))
        for i in reversed(order) if reverse else order:
            outs[i] = acc
            acc = [gains[i][h] * acc[h] + parts[i][h] for h in range(nhead)]
        return outs, acc

    def zeros():
        return [jnp.zeros((QUARTER, HDIM), F32) for _ in range(nhead)]

    def gains_of(ref, count):
        return [[jnp.exp(ref[i][h : h + 1, :]) for h in range(nhead)] for i in range(count)]

    def parts_of(ref, n, count):
        return [[ref[n, i, h].astype(F32) for h in range(nhead)] for i in range(count)]

    def scan_x(n, states):
        for q in range(NX):
            for h in range(nhead):
                loc[n, q, h] = states[h][q * QUARTER : (q + 1) * QUARTER].astype(BF16)
        for d in (2, 1, 3):
            xx = lax.rem(x + d, NX)
            device = to_ctx(ctx_at(z, y, xx))
            remote(loc.at[n, xx], p1.at[n, x], s_send.at[n, 0], s_recv.at[n, 0], device).start()
            if n == 0:
                remote(tx.at[x], tx.at[x], t_send.at[0], t_recv.at[0], device).start()
        sent(loc.at[n, pl.ds(0, NX - 1)], s_send.at[n, 0])
        if n == 0:
            sent(tx.at[pl.ds(0, NX - 1)], t_send.at[0])
        p1[n, x] = loc[n, x]

    def scan_y(n):
        arrived(p1.at[n, pl.ds(0, NX - 1)], s_recv.at[n, 0])
        if n == 0:
            arrived(tx.at[pl.ds(0, NX - 1)], t_recv.at[0])
            by[y] = tx[0] + tx[1] + tx[2] + tx[3]
        _, total = line_fold(parts_of(p1, n, NX), gains_of(tx, NX), n == 1, zeros())
        for h in range(nhead):
            p2[n, y, h] = total[h].astype(BF16)
        device = to_ctx(ctx_at(z, 1 - y, x))
        send(p2.at[n, y], s_send.at[n, 1], s_recv.at[n, 1], device)
        if n == 0:
            send(by.at[y], t_send.at[1], t_recv.at[1], device)

    def scan_z(n):
        arrived(p2.at[n, 1 - y], s_recv.at[n, 1])
        if n == 0:
            arrived(by.at[1 - y], t_recv.at[1])
            bz[z] = by[0] + by[1]
        _, total = line_fold(parts_of(p2, n, NY), gains_of(by, NY), n == 1, zeros())
        for h in range(nhead):
            p3[n, z, h] = total[h].astype(BF16)
        for d in (4, 3, 5, 2, 6, 1, 7):
            device = to_ctx(ctx_at(lax.rem(z + d, NZ), y, x))
            remote(p3.at[n, z], p3.at[n, z], s_send.at[n, 2], s_recv.at[n, 2], device).start()
            if n == 0:
                remote(bz.at[z], bz.at[z], t_send.at[2], t_recv.at[2], device).start()
        sent(p3.at[n, pl.ds(0, NZ - 1)], s_send.at[n, 2])
        if n == 0:
            sent(bz.at[pl.ds(0, NZ - 1)], t_send.at[2])

    def scan_back(n):
        arrived(p3.at[n, pl.ds(0, NZ - 1)], s_recv.at[n, 2])
        if n == 0:
            arrived(bz.at[pl.ds(0, NZ - 1)], t_recv.at[2])
        reverse = n == 1
        gains = gains_of(bz, NZ)
        parts = parts_of(p3, n, NZ)
        acc = zeros()
        for i in reversed(range(NZ)) if reverse else range(NZ):
            use = z < i if reverse else z > i
            keep = jnp.where(use, 1.0, 0.0)
            acc = [
                acc[h] * (1.0 - keep + keep * gains[i][h]) + keep * parts[i][h]
                for h in range(nhead)
            ]
        outs, _ = line_fold(parts_of(p2, n, NY), gains_of(by, NY), reverse, acc)
        first = jnp.where(y == 0, 1.0, 0.0)
        acc = [first * outs[0][h] + (1.0 - first) * outs[1][h] for h in range(nhead)]
        outs, _ = line_fold(parts_of(p1, n, NX), gains_of(tx, NX), reverse, acc)
        for i in range(NX):
            for h in range(nhead):
                p4s[n, i, h] = outs[i][h].astype(BF16)
        for d in (2, 1, 3):
            xx = lax.rem(x + d, NX)
            remote(p4s.at[n, xx], p4.at[n, x], s_send.at[n, 3], s_recv.at[n, 3],
                   to_ctx(ctx_at(z, y, xx))).start()
        sent(p4s.at[n, pl.ds(0, NX - 1)], s_send.at[n, 3])
        p4[n, x] = p4s[n, x]

    def scan_end(n):
        arrived(p4.at[n, pl.ds(0, NX - 1)], s_recv.at[n, 3])
        return [
            jnp.concatenate([p4[n, q, h] for q in range(NX)], axis=0) for h in range(nhead)
        ]

    def cols(h):
        return slice(h * HDIM, (h + 1) * HDIM)

    local[5].wait()
    lg[0:nhead, :] = logs[...]
    log_rows = lg[...]
    gate = jnp.sqrt(one_less_exp(2.0 * log_rows))
    lane = lax.broadcasted_iota(jnp.int32, log_rows.shape, 1)
    cumul = log_rows
    shift = 1
    while shift < tokens:
        cumul = cumul + jnp.where(lane >= shift, pltpu.roll(cumul, shift, 1), 0.0)
        shift *= 2
    total = cumul[:, tokens - 1 : tokens]
    tx[x] = jnp.broadcast_to(total, (8, HDIM))
    rows[0:8, :] = gate
    rows[8:16, :] = scale * jnp.exp(cumul)
    rows[16:24, :] = jnp.exp(total - cumul)
    rows[24:32, :] = cumul
    columns = jnp.transpose(rows[...])
    gate_c = [columns[:, h : h + 1] for h in range(nhead)]
    head_c = [columns[:, 8 + h : 9 + h] for h in range(nhead)]
    tail_c = [columns[:, 16 + h : 17 + h] for h in range(nhead)]
    cumul_c = [columns[:, 24 + h : 25 + h] for h in range(nhead)]

    local[2].wait()
    local[3].wait()
    states = []
    for h in range(nhead):
        scaled = (gate_c[h] * keys[:, cols(h)].astype(F32)).astype(BF16)
        sk[:, cols(h)] = scaled
        decayed = (tail_c[h] * scaled.astype(F32)).astype(BF16)
        states.append(mm_tn(decayed, values[:, cols(h)]))

    pl.semaphore_wait(barrier, len(partners))
    weights_y()
    local[0].wait()
    def h_issue_by(which, k):
        if k < chunks:
            @pl.when(core == which)
            def _():
                h_issue(k)

    chunks = h_recv.shape[1]
    for which, ahead in enumerate(AHEAD):
        for k in range(ahead):
            h_issue_by(which, k)
    scan_x(0, states)

    local[4].wait()
    block = 128
    tri = lax.broadcasted_iota(jnp.int32, (block, block), 0) >= lax.broadcasted_iota(
        jnp.int32, (block, block), 1
    )
    for h in range(nhead):
        cumul_r = rows[24 + h : 25 + h, :]
        for t0 in range(0, tokens, block):
            t = slice(t0, t0 + block)
            for s0 in range(0, t0 + block, block):
                s = slice(s0, s0 + block)
                spread = cumul_c[h][t] - cumul_r[:, s]
                if s0 == t0:
                    decays = jnp.where(tri, jnp.exp(jnp.where(tri, spread, 0.0)) * scale, 0.0)
                else:
                    decays = jnp.exp(spread) * scale
                dots = mm_nt(d_out[t, cols(h)], values[s, cols(h)])
                dec[h, t, s] = decays
                wdv[h, t, s] = (decays * dots).astype(BF16)

    def intra_query(h, t0):
        t = slice(t0, t0 + block)
        return mm(wdv[h, t, 0 : t0 + block], sk[0 : t0 + block, cols(h)])

    weights_z()
    scan_y(0)

    def h_product(k0, k1):
        h_finish(k0 // 2)
        t = slice(k0 * h_step, k1 * h_step)
        acc = jnp.zeros((t.stop - t.start, width), F32)
        for b in range(2 * NP):
            acc = acc + mm(hid[b, t, :], w[b * feats : (b + 1) * feats, :])
        query[t, :] = acc.astype(BF16)

    def h_chunk(k):
        h_forward(k)
        for which, ahead in enumerate(AHEAD):
            h_issue_by(which, k + ahead)

    h_chunk(0)
    h_chunk(1)
    scan_z(0)
    h_product(0, 2)
    h_chunk(2)
    weights_x()
    h_chunk(3)
    scan_back(0)
    h_product(2, 4)
    h_chunk(4)
    h_chunk(5)
    h_product(4, 6)

    state_in = scan_end(0)
    for h in range(nhead):
        for t0 in range(0, tokens, block):
            t = slice(t0, t0 + block)
            carry = mm_nt(d_out[t, cols(h)], state_in[h])
            out = intra_query(h, t0) + head_c[h][t] * carry
            dqf[head, t, cols(h)] = out.astype(BF16)

    h_chunk(6)
    h_chunk(7)
    q_issue(0)
    h_product(6, 8)

    adjoints = []
    for h in range(nhead):
        decayed = (head_c[h] * query[:, cols(h)].astype(F32)).astype(BF16)
        adjoints.append(mm_tn(decayed, d_out[:, cols(h)]))
    scan_x(1, adjoints)
    q_chunks = q_recv.shape[1]
    q_issue(1)

    outs = []

    def out_copy(src, dst):
        copy = pltpu.make_async_copy(src, dst, out_sem.at[len(outs)])
        copy.start()
        outs.append(copy)

    def q_product(k):
        q_finish(k)
        t = slice(k * q_step, (k + 1) * q_step)
        acc = jnp.zeros((q_step, feats), F32)
        for b in range(2 * NP):
            acc = acc + mm_nt(dqf[b, t, :], wr[b])
        dh_ref[t, :] = acc.astype(BF16)
        out_copy(dh_ref.at[t, :], dh_hbm.at[t, :])

    scan_y(1)
    for k in range(2, q_chunks):
        q_issue(k)
    weights_forward()

    for h in range(nhead):
        for s0 in range(0, tokens, block):
            s = slice(s0, s0 + block)
            later = slice(s0, tokens)
            scores = mm_nt(query[later, cols(h)], sk[s, cols(h)])
            weight = (dec[h, later, s] * scores).astype(BF16)
            sums[0, s, cols(h)] = mm_tn(wdv[h, later, s], query[later, cols(h)])
            sums[1, s, cols(h)] = mm_tn(weight, d_out[later, cols(h)])

    q_forward(0)
    scan_z(1)
    q_forward(1)
    q_forward(2)
    scan_back(1)
    weights_end()
    q_product(0)
    q_forward(3)
    q_product(1)
    q_product(2)
    adjoint_in = scan_end(1)
    for h in range(nhead):
        carry_keys = mm_nt(values[:, cols(h)], adjoint_in[h])
        carry_values = mm(sk[:, cols(h)], adjoint_in[h])
        d_scaled = sums[0, :, cols(h)] + tail_c[h] * carry_keys
        dk_ref[:, cols(h)] = (gate_c[h] * d_scaled).astype(BF16)
        dv_ref[:, cols(h)] = (sums[1, :, cols(h)] + tail_c[h] * carry_values).astype(BF16)
    out_copy(dk_ref, dk_hbm)
    out_copy(dv_ref, dv_hbm)
    q_product(3)
    h_close()
    q_close()
    drain()
    for copy in outs:
        copy.wait()


def finish(*refs):
    n = 3
    sems = refs[2 * n]
    copies = [pltpu.make_async_copy(refs[i], refs[n + i], sems.at[i]) for i in range(n)]
    for copy in copies:
        copy.start()
    for copy in copies:
        copy.wait()


def body(hidden, w_query, keys, values, d_out, log_decay):
    tokens, feats = hidden.shape
    width = w_query.shape[1]
    nhead = width // HDIM
    groups = 2 * NP
    h_chunks, q_chunks = 8, 4
    dma = pltpu.SemaphoreType.DMA
    vmem = pltpu.VMEM
    scratch = [
        vmem((nhead, tokens), F32),
        vmem((tokens, width), BF16),
        vmem((tokens, width), BF16),
        vmem((tokens, width), BF16),
        vmem((tokens, feats), BF16),
        vmem((tokens, width), BF16),
        vmem((tokens, width), BF16),
        vmem((groups, tokens, feats), BF16),
        vmem(w_query.shape, BF16),
        vmem((groups, feats, width), BF16),
        vmem((groups, tokens, width), BF16),
        vmem((tokens, width), BF16),
        vmem((tokens, width), BF16),
        vmem((8, tokens), F32),
        vmem((128, tokens), F32),
        vmem((nhead, tokens, tokens), F32),
        vmem((nhead, tokens, tokens), BF16),
        vmem((2, NX, nhead, QUARTER, HDIM), BF16),
        vmem((2, NX, nhead, QUARTER, HDIM), BF16),
        vmem((2, NY, nhead, QUARTER, HDIM), BF16),
        vmem((2, NZ, nhead, QUARTER, HDIM), BF16),
        vmem((2, NX, nhead, QUARTER, HDIM), BF16),
        vmem((2, NX, nhead, QUARTER, HDIM), BF16),
        vmem((NX, 8, HDIM), F32),
        vmem((NY, 8, HDIM), F32),
        vmem((NZ, 8, HDIM), F32),
        vmem((2, tokens, width), F32),
        dma((6,)),
        dma((q_chunks + 2,)),
    ]
    for chunks in (h_chunks, q_chunks):
        scratch += [dma((9,)), dma((NP, chunks)), dma((4,))]
    scratch += [dma((1,))] * 4 + [dma((2,))] * 4
    scratch += [dma((2, 4)), dma((2, 4)), dma((3,)), dma((3,))]
    anywhere = pl.BlockSpec(memory_space=pl.ANY)
    shapes = (
        jax.ShapeDtypeStruct((tokens, feats), BF16),
        jax.ShapeDtypeStruct((tokens, width), BF16),
        jax.ShapeDtypeStruct((tokens, width), BF16),
    )
    results = pl.pallas_call(
        kernel,
        out_shape=shapes,
        in_specs=[pl.BlockSpec(memory_space=pltpu.HBM)] * 6,
        out_specs=(anywhere,) * 3,
        scratch_shapes=scratch,
        compiler_params=pltpu.CompilerParams(
            collective_id=0, has_side_effects=True, vmem_limit_bytes=32 * 1024 * 1024
        ),
    )(*(pltpu.with_memory_space_constraint(a, pltpu.HBM) for a in (hidden, w_query, keys, values, d_out, log_decay.T)))
    return pl.pallas_call(
        finish,
        out_shape=shapes,
        in_specs=[anywhere] * 3,
        out_specs=(anywhere,) * 3,
        scratch_shapes=[dma((3,))],
        compiler_params=pltpu.CompilerParams(vmem_limit_bytes=4 * 1024 * 1024),
    )(*results)


def solution(mesh):
    return jax.shard_map(
        body,
        mesh=mesh,
        in_specs=(
            P("ctx", "head"),
            P(None, "head"),
            P("ctx", "head"),
            P("ctx", "head"),
            P("ctx", "head"),
            P("ctx", "head"),
        ),
        out_specs=(P("ctx", "head"), P("ctx", "head"), P("ctx", "head")),
        check_vma=False,
    )
```
